256 devices in a mesh: doc: 64 (over z, y, core), tp: 4 (over x).
Axes of the slice: x: 4, y: 4, z: 8, core: 2. Of those that a mesh axis runs over, the one named last changes fastest.
Arguments:
- storage: bfloat16 [32768, 3584], P('doc', 'tp'), may hold values from -40 to 40
- row_doc: int32 [32768], P('doc'), may hold values from -1 to 63, as said below
- row_pos: int32 [32768], P('doc'), may hold values from -1 to 511, as said below
- doc_len: int32 [64], replicated, may hold values from 64 to 512, as said below
- partner: int32 [64], replicated, may hold values from 0 to 63, as said below
- norm_gain: bfloat16 [3584], replicated, may hold values from 0.25 to 1.75
- qkv_weight: bfloat16 [3584, 4608], P('doc', 'tp'), may hold values from -0.09375 to 0.09375
- qkv_bias: bfloat16 [4608], P('tp'), may hold values from -24 to 24
Outputs:
- attention: bfloat16 [65536, 3584], P('doc', 'tp')
The draws below stay inside these ranges and needn't reach their ends.
Inputs may be any that keep to these rules, and one draw needn't show every extreme that they name: `row_doc`: the rows 0 to doc_len[d] - 1 of each document d are stored exactly once over all devices, one to a slot; -1 marks an empty slot. One device stores at most 8 rows of any one document, and exactly 8 rows of a document of 512 tokens. `row_pos`: -1 for an empty slot. `doc_len`: some document has 512 tokens and some has 64. partner[partner[d]] = d and partner[d] != d.
All inputs are finite; a program needn't handle non-finite values.
Results may differ from the reference program's by a relative error of at most 0.008.
The reference program's roundings to bfloat16 on the way count: a program that leaves them out, or rounds other values in their place, can miss the bound.
Values may be sent and summed in bfloat16 or wider, within the bound.
A program may use at most 64 MiB of HBM per device.

```python
import jax
import jax.numpy as jnp
from jax import lax

D = 3584
HEADS = 28
KVH = 4
HD = 128
HALF = 512
DOCS = 64
SEQ = 1024
COLS = 4608
N_TP = 4


def doc_lengths(key):
    length_key, pick_key = jax.random.split(jax.random.fold_in(key, 11))
    lengths = jax.random.randint(length_key, (DOCS,), HALF // 8, HALF + 1)
    longest_length = jax.random.randint(pick_key, (), 0, DOCS)
    doc_ids = jnp.arange(DOCS)
    lengths = jnp.where(doc_ids == longest_length, HALF, lengths)
    lengths = jnp.where(doc_ids == (longest_length + 1) % DOCS, HALF // 8, lengths)
    return lengths.astype(jnp.int32)


def owner_permutation(owner_key):
    return jax.random.permutation(owner_key, HALF)


def storage_map(key):
    lengths = doc_lengths(key)
    rotate_key, slot_key = jax.random.split(jax.random.fold_in(key, 12))
    rotation = jax.random.randint(rotate_key, (DOCS,), 0, DOCS)
    positions = jnp.arange(HALF)
    valid = (positions[None, :] < lengths[:, None]).reshape(-1)
    owners = ((rotation[:, None] + positions[None, :]) % DOCS).reshape(-1)
    onehot = ((owners[:, None] == jnp.arange(DOCS)[None, :]) & valid[:, None]).astype(jnp.int32)
    ranks = jnp.sum(jnp.cumsum(onehot, axis=0) * onehot, axis=1) - 1
    shuffles = jax.vmap(owner_permutation)(jax.random.split(slot_key, DOCS))
    slots = shuffles[owners, jnp.maximum(ranks, 0)]
    target = jnp.where(valid, owners * HALF + slots, DOCS * HALF)
    doc_of_row = jnp.repeat(jnp.arange(DOCS), HALF).astype(jnp.int32)
    pos_of_row = jnp.tile(positions, DOCS).astype(jnp.int32)
    row_doc = jnp.full((DOCS * HALF,), -1, jnp.int32).at[target].set(doc_of_row, mode='drop')
    row_pos = jnp.full((DOCS * HALF,), -1, jnp.int32).at[target].set(pos_of_row, mode='drop')
    return (row_doc, row_pos)


def draw_row_doc(key, part):
    return storage_map(key)[0]


def draw_row_pos(key, part):
    return storage_map(key)[1]


def draw_doc_len(key, part):
    return doc_lengths(key)


def draw_partner(key, part):
    order = jax.random.permutation(jax.random.fold_in(key, 13), DOCS).astype(jnp.int32)
    paired = order.reshape(DOCS // 2, 2)
    partner = jnp.zeros((DOCS,), jnp.int32).at[paired[:, 0]].set(paired[:, 1])
    return partner.at[paired[:, 1]].set(paired[:, 0])


def draw_storage(key, part):
    base_key, row_key, col_key = jax.random.split(jax.random.fold_in(key, 21), 3)
    total_rows = DOCS * HALF
    row_scale = jnp.exp(jax.random.uniform(row_key, (total_rows, 1), jnp.float32, -1.2, 1.2))
    col_scale = jnp.exp(jax.random.uniform(col_key, (1, D), jnp.float32, -1.2, 1.2))
    base = jax.random.normal(base_key, (total_rows, D), jnp.float32)
    return jnp.clip(base * row_scale * col_scale, -40.0, 40.0).astype(jnp.bfloat16)


def draw_qkv_bias(key, part):
    base_key = jax.random.fold_in(jax.random.fold_in(key, 31), 0)
    base = 0.5 * jax.random.normal(base_key, (COLS,), jnp.float32)
    return jnp.clip(base, -24.0, 24.0).astype(jnp.bfloat16)


def block_scale(own_key, dims, shards, low, top_value):
    factor_of, own = 1.0, jax.random.fold_in(own_key, 6)
    for dim, blocks in shards:
        heights = jnp.exp(jax.random.uniform(jax.random.fold_in(own, dim), (blocks,), jnp.float32, low / len(shards), top_value / len(shards)))
        factor_of = factor_of * jnp.repeat(heights, dims[dim] // blocks).reshape([-1 if axis == dim else 1 for axis in range(len(dims))])
    return factor_of


def scatter_about(stream_key, extent, scale, bound, pieces=(), kind=jnp.bfloat16):
    array = jax.random.normal(stream_key, extent, jnp.float32) * scale
    if len(pieces) > 0:
        array = block_scale(stream_key, extent, pieces, -0.22, 0.18) * array
    return jnp.clip(array, min=-bound, max=bound).astype(kind)


def setup_inputs(seed: int = 0) -> dict:
    key_list = jax.random.split(jax.random.key(seed), 9)
    storage = draw_storage(jax.random.fold_in(key_list[8], 71), 0)
    row_doc = draw_row_doc(jax.random.fold_in(key_list[8], 71), 0)
    row_pos = draw_row_pos(jax.random.fold_in(key_list[8], 71), 0)
    doc_len = draw_doc_len(jax.random.fold_in(key_list[8], 71), 0)
    partner = draw_partner(jax.random.fold_in(key_list[8], 71), 0)
    norm_gain = jnp.clip(1.0 + 0.15 * jax.random.normal(key_list[5], (D,), jnp.float32), 0.25, 1.75).astype(jnp.bfloat16)
    qkv_weight = scatter_about(key_list[6], (D, COLS), D ** -0.5, 0.09375, ((0, 64), (1, 4)))
    qkv_bias = draw_qkv_bias(jax.random.fold_in(key_list[8], 71), 0)
    return {"storage": storage, "row_doc": row_doc, "row_pos": row_pos, "doc_len": doc_len, "partner": partner, "norm_gain": norm_gain, "qkv_weight": qkv_weight, "qkv_bias": qkv_bias}


ROPE_BASE = 1000000.0
EPSILON = 1e-06

def pairing(partner):
    doc_ids = jnp.arange(partner.shape[0], dtype=jnp.int32)
    first_flag = (doc_ids < partner).astype(jnp.int32)
    before = jnp.cumsum(first_flag) - first_flag
    low_doc = jnp.minimum(doc_ids, partner)
    pick_mask = (low_doc[:, None] == doc_ids[None, :]).astype(jnp.int32)
    pair_index = lax.optimization_barrier(jnp.sum(pick_mask * before[None, :], axis=1))
    scorer = 2 * pair_index + 1 - first_flag
    match_mask = (scorer[None, :] == doc_ids[:, None]).astype(jnp.int32)
    own_doc = lax.optimization_barrier(jnp.sum(match_mask * doc_ids[None, :], axis=1))
    return (scorer, own_doc)

def rope_tables(length, head_dim):
    half_dim = head_dim // 2
    freq_ids = jnp.arange(half_dim, dtype=jnp.float32)
    inv_freq = jnp.exp(-(2.0 * freq_ids / head_dim) * jnp.log(jnp.float32(ROPE_BASE)))
    angles = jnp.arange(length, dtype=jnp.float32)[:, None] * inv_freq[None, :]
    cosine = jnp.concatenate([jnp.cos(angles), jnp.cos(angles)], axis=1)
    sine_table = jnp.concatenate([jnp.sin(angles), jnp.sin(angles)], axis=1)
    return (cosine, sine_table)

def rotate(heads, cosine, sine_table):
    widened = heads.astype(jnp.float32)
    half_dim = widened.shape[-1] // 2
    turned = jnp.concatenate([-widened[..., half_dim:], widened[..., :half_dim]], axis=-1)
    return (widened * cosine[:, None, :] + turned * sine_table[:, None, :]).astype(jnp.bfloat16)

def rms_norm(row_values, norm_gain):
    widened = row_values.astype(jnp.float32)
    inv_rms = lax.rsqrt(lax.optimization_barrier(jnp.mean(widened * widened, axis=-1, keepdims=True)) + EPSILON)
    return (widened * inv_rms * norm_gain.astype(jnp.float32)).astype(jnp.bfloat16)

def attend_ref(queries, key_heads, value_heads, total_len):
    length, q_heads, head_dim = queries.shape
    kv_heads = key_heads.shape[1]
    grouped = queries.reshape(length, kv_heads, q_heads // kv_heads, head_dim).astype(jnp.float32)
    scores = jnp.einsum('qkgd,skd->kgqs', grouped, key_heads.astype(jnp.float32)) / jnp.sqrt(jnp.float32(head_dim))
    row_ids = jnp.arange(length, dtype=jnp.int32)[:, None]
    col_ids = jnp.arange(length, dtype=jnp.int32)[None, :]
    allowed = (col_ids <= row_ids) & (col_ids < total_len)
    scores = jnp.where(allowed, scores, -jnp.inf)
    largest = lax.optimization_barrier(jnp.max(scores, axis=-1, keepdims=True))
    exponent = jnp.exp(scores - largest)
    probabilities = (exponent / lax.optimization_barrier(jnp.sum(exponent, axis=-1, keepdims=True))).astype(jnp.bfloat16)
    mixture = jnp.einsum('kgqs,skd->qkgd', probabilities.astype(jnp.float32), value_heads.astype(jnp.float32))
    live_rows = (jnp.arange(length, dtype=jnp.int32) < total_len)[:, None, None, None]
    mixture = jnp.where(live_rows, mixture, 0.0)
    return mixture.astype(jnp.bfloat16).reshape(length, q_heads * head_dim)

def head_attention(projected, total_len, cosine, sine_table, q_heads, kv_heads):
    length = projected.shape[0]
    queries = projected[:, :q_heads * HD].reshape(length, q_heads, HD)
    key_heads = projected[:, q_heads * HD:(q_heads + kv_heads) * HD].reshape(length, kv_heads, HD)
    value_heads = projected[:, (q_heads + kv_heads) * HD:].reshape(length, kv_heads, HD)
    queries = rotate(queries, cosine, sine_table)
    key_heads = rotate(key_heads, cosine, sine_table)
    return attend_ref(queries, key_heads, value_heads, total_len)

def reference(storage, row_doc, row_pos, doc_len, partner, norm_gain, qkv_weight, qkv_bias):
    doc_count = doc_len.shape[0]
    feature_count = storage.shape[1]
    scorer, own_doc = pairing(partner)
    target = jnp.where(row_doc >= 0, row_doc * HALF + row_pos, doc_count * HALF).astype(jnp.int32)
    doc_rows = jnp.zeros((doc_count * HALF, feature_count), jnp.bfloat16).at[target].set(storage, mode='drop')
    doc_rows = doc_rows.reshape(doc_count, HALF, feature_count)
    shard_cols = qkv_weight.shape[1] // N_TP
    q_heads = HEADS // N_TP
    kv_heads = KVH // N_TP
    cosine, sine_table = rope_tables(SEQ, HD)

    def score_one(scorer_id):
        first_doc = own_doc[scorer_id]
        second_doc = partner[first_doc]
        first_len = doc_len[first_doc].astype(jnp.int32)
        total_len = first_len + doc_len[second_doc]
        joint_rows = jnp.concatenate([doc_rows[first_doc], jnp.zeros((HALF, feature_count), jnp.bfloat16)], axis=0)
        joint_rows = lax.dynamic_update_slice(joint_rows, doc_rows[second_doc], (first_len, jnp.int32(0)))
        normed = rms_norm(joint_rows, norm_gain)
        outputs = []
        for shard_id in range(N_TP):
            col_start = shard_id * shard_cols
            col_stop = col_start + shard_cols
            product = jnp.dot(normed, qkv_weight[:, col_start:col_stop], preferred_element_type=jnp.float32)
            projected = (product + qkv_bias[col_start:col_stop].astype(jnp.float32)).astype(jnp.bfloat16)
            outputs.append(head_attention(projected, total_len, cosine, sine_table, q_heads, kv_heads))
        return jnp.concatenate(outputs, axis=1)
    result = lax.map(score_one, jnp.arange(doc_count, dtype=jnp.int32))
    return result.reshape(doc_count * SEQ, HEADS * HD)
```

```python
import jax
import jax.numpy as jnp
from jax import lax
from jax.sharding import PartitionSpec as P

HEADS = 28
KVH = 4
HD = 128
HALF = 512


ROPE_BASE = 1000000.0
EPSILON = 1e-06
BLOCK_ROWS = 512


def from_partner(value, axis, stride):
    mask = 2**stride
    pairs = [(source, source ^ mask) for source in range(lax.axis_size(axis))]
    return lax.ppermute(value, axis, pairs)


def pairing(partner):
    doc_ids = jnp.arange(partner.shape[0], dtype=jnp.int32)
    first_flag = (doc_ids < partner).astype(jnp.int32)
    before = jnp.cumsum(first_flag) - first_flag
    low_doc = jnp.minimum(doc_ids, partner)
    pick_mask = (low_doc[:, None] == doc_ids[None, :]).astype(jnp.int32)
    pair_index = jnp.sum(pick_mask * before[None, :], axis=1)
    scorer = 2 * pair_index + 1 - first_flag
    match_mask = (scorer[None, :] == doc_ids[:, None]).astype(jnp.int32)
    own_doc = jnp.sum(match_mask * doc_ids[None, :], axis=1)
    return (scorer, own_doc)


def rope_tables(length, head_dim):
    half_dim = head_dim // 2
    freq_ids = jnp.arange(half_dim, dtype=jnp.float32)
    inv_freq = jnp.exp(-(2.0 * freq_ids / head_dim) * jnp.log(jnp.float32(ROPE_BASE)))
    angles = jnp.arange(length, dtype=jnp.float32)[:, None] * inv_freq[None, :]
    cosine = jnp.concatenate([jnp.cos(angles), jnp.cos(angles)], axis=1)
    sine_table = jnp.concatenate([jnp.sin(angles), jnp.sin(angles)], axis=1)
    return (cosine, sine_table)


def rotate(heads, cosine, sine_table):
    widened = heads.astype(jnp.float32)
    half_dim = widened.shape[-1] // 2
    turned = jnp.concatenate([-widened[..., half_dim:], widened[..., :half_dim]], axis=-1)
    return (widened * cosine[:, None, :] + turned * sine_table[:, None, :]).astype(jnp.bfloat16)


def rms_norm(row_values, norm_gain):
    widened = row_values.astype(jnp.float32)
    inv_rms = lax.rsqrt(jnp.mean(widened * widened, axis=-1, keepdims=True) + EPSILON)
    return (widened * inv_rms * norm_gain.astype(jnp.float32)).astype(jnp.bfloat16)


def place_rows(values, dest_index, length):
    blank_rows = jnp.zeros((length,) + values.shape[1:], values.dtype)
    return blank_rows.at[dest_index].set(values, mode="drop")


def assemble(first_part, second_part, first_len):
    padded = jnp.concatenate([first_part, jnp.zeros_like(second_part)], axis=0)
    return lax.dynamic_update_slice(padded, second_part, (first_len, jnp.int32(0)))


def attention(projected, total_len, q_heads, kv_heads, head_dim):
    length = projected.shape[0]
    cosine, sine_table = rope_tables(length, head_dim)
    queries = rotate(
        projected[:, : q_heads * head_dim].reshape(length, q_heads, head_dim), cosine, sine_table
    )
    key_heads = rotate(
        projected[:, q_heads * head_dim : (q_heads + kv_heads) * head_dim].reshape(
            length, kv_heads, head_dim
        ),
        cosine,
        sine_table,
    )
    value_heads = projected[:, (q_heads + kv_heads) * head_dim :].reshape(
        length, kv_heads, head_dim
    )
    grouped = queries.reshape(length, kv_heads, q_heads // kv_heads, head_dim)
    block_length = min(BLOCK_ROWS, length)
    root_dim = jnp.sqrt(jnp.float32(head_dim))
    pieces = []
    for row_start in range(0, length, block_length):
        row_stop = row_start + block_length
        scores = (
            jnp.einsum(
                "qkgd,skd->kgqs",
                grouped[row_start:row_stop],
                key_heads[:row_stop],
                preferred_element_type=jnp.float32,
            )
            / root_dim
        )
        row_ids = jnp.arange(row_start, row_stop, dtype=jnp.int32)[:, None]
        col_ids = jnp.arange(row_stop, dtype=jnp.int32)[None, :]
        allowed = (col_ids <= row_ids) & (col_ids < total_len)
        scores = jnp.where(allowed, scores, -jnp.inf)
        largest = jnp.max(scores, axis=-1, keepdims=True)
        exponent = jnp.exp(scores - largest)
        probabilities = (exponent / jnp.sum(exponent, axis=-1, keepdims=True)).astype(jnp.bfloat16)
        mixture = jnp.einsum(
            "kgqs,skd->qkgd",
            probabilities,
            value_heads[:row_stop],
            preferred_element_type=jnp.float32,
        )
        live_rows = (jnp.arange(row_start, row_stop, dtype=jnp.int32) < total_len)[
            :, None, None, None
        ]
        mixture = jnp.where(live_rows, mixture, 0.0)
        pieces.append(mixture.astype(jnp.bfloat16).reshape(block_length, q_heads * head_dim))
    return jnp.concatenate(pieces, axis=0)


def shards(storage, row_doc, row_pos, doc_len, partner, norm_gain, qkv_weight, qkv_bias):
    pair_count = lax.axis_size("pair")
    doc_count = 2 * pair_count
    core = lax.axis_index("core")
    me_index = lax.axis_index("pair") * 2 + core
    half_rows = HALF
    per_dest = half_rows // doc_count
    scorer, own_doc = pairing(partner)
    doc_ids = jnp.arange(doc_count, dtype=jnp.int32)
    first_doc = jnp.sum(jnp.where(doc_ids == me_index, own_doc, 0))
    second_doc = jnp.sum(jnp.where(doc_ids == first_doc, partner, 0))
    first_len = jnp.sum(jnp.where(doc_ids == first_doc, doc_len, 0))
    second_len = jnp.sum(jnp.where(doc_ids == second_doc, doc_len, 0))
    total_len = first_len + second_len
    stored = row_doc >= 0
    dest_scorer = jnp.sum(
        jnp.where(row_doc[:, None] == doc_ids[None, :], scorer[None, :], 0), axis=1
    )
    onehot = ((dest_scorer[:, None] == doc_ids[None, :]) & stored[:, None]).astype(jnp.int32)
    dest_rank = jnp.sum(jnp.cumsum(onehot, axis=0) * onehot, axis=1) - 1
    dest_index = jnp.where(stored, dest_scorer * per_dest + dest_rank, doc_count * per_dest)
    send_rows = place_rows(storage, dest_index, doc_count * per_dest).reshape(
        doc_count, per_dest, storage.shape[1]
    )
    send_pos = (
        jnp.full((doc_count * per_dest,), half_rows, jnp.int32)
        .at[dest_index]
        .set(row_pos, mode="drop")
    )
    send_pos = send_pos.reshape(doc_count, per_dest)
    doc_axes = ("pair", "core")
    got_rows, got_pos = (
        lax.all_to_all(send_rows, doc_axes, split_axis=0, concat_axis=0, tiled=True),
        lax.all_to_all(send_pos, doc_axes, split_axis=0, concat_axis=0, tiled=True),
    )
    own_rows = place_rows(
        got_rows.reshape(doc_count * per_dest, storage.shape[1]), got_pos.reshape(-1), half_rows
    )
    q_heads = HEADS // lax.axis_size("tp")
    kv_heads = KVH // lax.axis_size("tp")
    bias_wide = qkv_bias.astype(jnp.float32)
    own_full = lax.all_gather(own_rows, "tp", axis=1, tiled=True)
    normed = rms_norm(own_full, norm_gain)
    mine = lax.all_gather(qkv_weight, "pair", axis=0, tiled=False)
    theirs = from_partner(mine, "core", 0)
    is_first = core == 0
    low = jnp.where(is_first, mine, theirs)
    high = jnp.where(is_first, theirs, mine)
    full_weight = jnp.stack([low, high], axis=1).reshape(-1, qkv_weight.shape[1])
    own_sum = jnp.dot(normed, full_weight, preferred_element_type=jnp.float32)
    own_proj = (own_sum + bias_wide).astype(jnp.bfloat16)
    other_proj = from_partner(own_proj, "core", 0)
    projected = assemble(own_proj, other_proj, first_len)
    return attention(projected, total_len, q_heads, kv_heads, HD)


def solution(mesh):
    doc_count, tp_count = mesh.shape["doc"], mesh.shape["tp"]
    split = jax.sharding.Mesh(
        mesh.devices.reshape(doc_count // 2, 2, tp_count), ("pair", "core", "tp")
    )
    rows = ("pair", "core")
    placed = (P(rows, "tp"), P(rows), P(rows), P(), P(), P(), P(rows, "tp"), P("tp"))
    return jax.shard_map(
        shards, mesh=split, in_specs=placed, out_specs=P(rows, "tp"), check_vma=False
    )
```

```python
import functools

import jax
import jax.numpy as jnp
from jax import lax
from jax.sharding import PartitionSpec as P
from jax.experimental import pallas as pl
from jax.experimental.pallas import tpu as pltpu
import numpy as np

HEADS = 28
KVH = 4
HD = 128
HALF = 512


ROPE_BASE = 1000000.0
EPSILON = 1e-06
BLOCK_ROWS = 512


def from_partner(value, axis, stride):
    mask = 2**stride
    pairs = [(source, source ^ mask) for source in range(lax.axis_size(axis))]
    return lax.ppermute(value, axis, pairs)


def pairing(partner):
    doc_ids = jnp.arange(partner.shape[0], dtype=jnp.int32)
    first_flag = (doc_ids < partner).astype(jnp.int32)
    before = jnp.cumsum(first_flag) - first_flag
    low_doc = jnp.minimum(doc_ids, partner)
    pick_mask = (low_doc[:, None] == doc_ids[None, :]).astype(jnp.int32)
    pair_index = jnp.sum(pick_mask * before[None, :], axis=1)
    scorer = 2 * pair_index + 1 - first_flag
    match_mask = (scorer[None, :] == doc_ids[:, None]).astype(jnp.int32)
    own_doc = jnp.sum(match_mask * doc_ids[None, :], axis=1)
    return (scorer, own_doc)


def rope_tables(length, head_dim):
    half_dim = head_dim // 2
    freq_ids = jnp.arange(half_dim, dtype=jnp.float32)
    inv_freq = jnp.exp(-(2.0 * freq_ids / head_dim) * jnp.log(jnp.float32(ROPE_BASE)))
    angles = jnp.arange(length, dtype=jnp.float32)[:, None] * inv_freq[None, :]
    cosine = jnp.concatenate([jnp.cos(angles), jnp.cos(angles)], axis=1)
    sine_table = jnp.concatenate([jnp.sin(angles), jnp.sin(angles)], axis=1)
    return (cosine, sine_table)


def rotate(heads, cosine, sine_table):
    widened = heads.astype(jnp.float32)
    half_dim = widened.shape[-1] // 2
    turned = jnp.concatenate([-widened[..., half_dim:], widened[..., :half_dim]], axis=-1)
    return (widened * cosine[:, None, :] + turned * sine_table[:, None, :]).astype(jnp.bfloat16)


def rms_norm(row_values, norm_gain):
    widened = row_values.astype(jnp.float32)
    inv_rms = lax.rsqrt(jnp.mean(widened * widened, axis=-1, keepdims=True) + EPSILON)
    return (widened * inv_rms * norm_gain.astype(jnp.float32)).astype(jnp.bfloat16)


def place_rows(values, dest_index, length):
    blank_rows = jnp.zeros((length,) + values.shape[1:], values.dtype)
    return blank_rows.at[dest_index].set(values, mode="drop")


def assemble(first_part, second_part, first_len):
    padded = jnp.concatenate([first_part, jnp.zeros_like(second_part)], axis=0)
    return lax.dynamic_update_slice(padded, second_part, (first_len, jnp.int32(0)))


QUERY_BLOCK = 256


def attend_kernel(total_ref, proj_ref, cos_ref, sin_ref, out_ref, keys_ref, *, q_heads, head_dim):
    length = proj_ref.shape[0]
    total = total_ref[0]
    root = np.float32(np.sqrt(np.float32(head_dim)))
    lane = lax.broadcasted_iota(jnp.int32, (1, head_dim), 1)
    half = head_dim // 2

    def rope(x, c, s):
        turned = pltpu.roll(x, half, 1)
        turned = jnp.where(lane < half, -turned, turned)
        return (x * c + turned * s).astype(jnp.bfloat16)

    key_col = q_heads * head_dim
    keys_ref[...] = rope(
        proj_ref[:, key_col : key_col + head_dim].astype(jnp.float32), cos_ref[...], sin_ref[...]
    )
    value_col = key_col + head_dim
    for start in range(0, length, QUERY_BLOCK):
        stop = start + QUERY_BLOCK
        c = cos_ref[start:stop, :]
        s = sin_ref[start:stop, :]
        row = start + lax.broadcasted_iota(jnp.int32, (QUERY_BLOCK, stop), 0)
        col = lax.broadcasted_iota(jnp.int32, (QUERY_BLOCK, stop), 1)
        allowed = (col <= row) & (col < total)
        live = (start + lax.broadcasted_iota(jnp.int32, (QUERY_BLOCK, 1), 0)) < total

        def one_head(h, carry):
            cols = pl.ds(pl.multiple_of(h * head_dim, head_dim), head_dim)
            q = rope(proj_ref[start:stop, cols].astype(jnp.float32), c, s)
            scores = lax.dot_general(
                q, keys_ref[0:stop, :], (((1,), (1,)), ((), ())),
                preferred_element_type=jnp.float32,
            ) / root
            scores = jnp.where(allowed, scores, -jnp.inf)
            largest = jnp.max(scores, axis=1, keepdims=True)
            exponent = jnp.exp(scores - largest)
            probs = (exponent / jnp.sum(exponent, axis=1, keepdims=True)).astype(jnp.bfloat16)
            mixture = jnp.dot(
                probs, proj_ref[0:stop, value_col : value_col + head_dim],
                preferred_element_type=jnp.float32,
            )
            out_ref[start:stop, cols] = jnp.where(live, mixture, 0.0).astype(out_ref.dtype)
            return carry

        lax.fori_loop(0, q_heads, one_head, 0)


def attention(projected, total_len, q_heads, kv_heads, head_dim):
    length = projected.shape[0]
    cosine, sine_table = rope_tables(length, head_dim)
    body = functools.partial(attend_kernel, q_heads=q_heads, head_dim=head_dim)
    flops = 2 * 2 * q_heads * head_dim * length * length // 2
    return pl.pallas_call(
        body,
        out_shape=jax.ShapeDtypeStruct((length, q_heads * head_dim), projected.dtype),
        in_specs=[
            pl.BlockSpec(memory_space=pltpu.SMEM),
            pl.BlockSpec(memory_space=pltpu.VMEM),
            pl.BlockSpec(memory_space=pltpu.VMEM),
            pl.BlockSpec(memory_space=pltpu.VMEM),
        ],
        out_specs=pl.BlockSpec(memory_space=pltpu.VMEM),
        scratch_shapes=[pltpu.VMEM((length, head_dim), jnp.bfloat16)],
        cost_estimate=pl.CostEstimate(
            flops=flops,
            transcendentals=q_heads * length * length // 2,
            bytes_accessed=projected.size * 2 + length * q_heads * head_dim * 2,
        ),
    )(total_len.reshape(1).astype(jnp.int32), projected, cosine, sine_table)


def shards(storage, row_doc, row_pos, doc_len, partner, norm_gain, qkv_weight, qkv_bias):
    pair_count = lax.axis_size("outer") * lax.axis_size("inner")
    doc_count = 2 * pair_count
    core = lax.axis_index("core")
    me_index = (lax.axis_index("outer") * lax.axis_size("inner") + lax.axis_index("inner")) * 2 + core
    half_rows = HALF
    per_dest = half_rows // doc_count
    scorer, own_doc = pairing(partner)
    doc_ids = jnp.arange(doc_count, dtype=jnp.int32)
    first_doc = jnp.sum(jnp.where(doc_ids == me_index, own_doc, 0))
    second_doc = jnp.sum(jnp.where(doc_ids == first_doc, partner, 0))
    first_len = jnp.sum(jnp.where(doc_ids == first_doc, doc_len, 0))
    second_len = jnp.sum(jnp.where(doc_ids == second_doc, doc_len, 0))
    total_len = first_len + second_len
    stored = row_doc >= 0
    dest_scorer = jnp.sum(
        jnp.where(row_doc[:, None] == doc_ids[None, :], scorer[None, :], 0), axis=1
    )
    onehot = ((dest_scorer[:, None] == doc_ids[None, :]) & stored[:, None]).astype(jnp.int32)
    dest_rank = jnp.sum(jnp.cumsum(onehot, axis=0) * onehot, axis=1) - 1
    dest_index = jnp.where(stored, dest_scorer * per_dest + dest_rank, doc_count * per_dest)
    send_rows = place_rows(storage, dest_index, doc_count * per_dest).reshape(
        doc_count, per_dest, storage.shape[1]
    )
    send_pos = (
        jnp.full((doc_count * per_dest,), half_rows, jnp.int32)
        .at[dest_index]
        .set(row_pos, mode="drop")
    )
    send_pos = send_pos.reshape(doc_count, per_dest)
    doc_axes = ("outer", "inner", "core")
    got_rows, got_pos = (
        lax.all_to_all(send_rows, doc_axes, split_axis=0, concat_axis=0, tiled=True),
        lax.all_to_all(send_pos, doc_axes, split_axis=0, concat_axis=0, tiled=True),
    )
    own_rows = place_rows(
        got_rows.reshape(doc_count * per_dest, storage.shape[1]), got_pos.reshape(-1), half_rows
    )
    q_heads = HEADS // lax.axis_size("tp")
    kv_heads = KVH // lax.axis_size("tp")
    bias_wide = qkv_bias.astype(jnp.float32)
    own_full = lax.all_gather(own_rows, "tp", axis=1, tiled=True)
    normed = rms_norm(own_full, norm_gain)
    mine = lax.all_gather(qkv_weight, "inner", axis=0, tiled=False)
    mine = lax.all_gather(mine, "outer", axis=0, tiled=False)
    mine = mine.reshape((-1,) + qkv_weight.shape)
    theirs = from_partner(mine, "core", 0)
    is_first = core == 0
    low = jnp.where(is_first, mine, theirs)
    high = jnp.where(is_first, theirs, mine)
    full_weight = jnp.stack([low, high], axis=1).reshape(-1, qkv_weight.shape[1])
    own_sum = jnp.dot(normed, full_weight, preferred_element_type=jnp.float32)
    own_proj = (own_sum + bias_wide).astype(jnp.bfloat16)
    other_proj = from_partner(own_proj, "core", 0)
    projected = assemble(own_proj, other_proj, first_len)
    return attention(projected, total_len, q_heads, kv_heads, HD)


def solution(mesh):
    doc_count, tp_count = mesh.shape["doc"], mesh.shape["tp"]
    pairs = doc_count // 2
    inner = 4 if pairs % 4 == 0 else 1
    split = jax.sharding.Mesh(
        mesh.devices.reshape(pairs // inner, inner, 2, tp_count), ("outer", "inner", "core", "tp")
    )
    rows = ("outer", "inner", "core")
    placed = (P(rows, "tp"), P(rows), P(rows), P(), P(), P(), P(rows, "tp"), P("tp"))
    return jax.shard_map(
        shards, mesh=split, in_specs=placed, out_specs=P(rows, "tp"), check_vma=False
    )
```
